128 devices in a mesh: dp: 128 (over x, y, z, core).
Axes of the slice: x: 4, y: 4, z: 4, core: 2. Of those that a mesh axis runs over, the one named last changes fastest.
Arguments:
- latents: bfloat16 [768, 256, 384], P('dp'), may hold values from -6 to 6
- conditioning: bfloat16 [768, 384], P('dp'), may hold values from -5 to 5
- latent_counts: int32 [128], P('dp'), may hold values from 1 to 6, as said below
- ada_weight: bfloat16 [384, 2304], P('dp'), may hold values from -0.3125 to 0.3125
- ada_bias: bfloat16 [2304], P('dp'), may hold values from -3 to 3
- qkv_weight: bfloat16 [384, 1152], P('dp'), may hold values from -0.3125 to 0.3125
- qv_bias: bfloat16 [2, 384], P(None, 'dp'), may hold values from -3 to 3
- proj_weight: bfloat16 [384, 384], P('dp'), may hold values from -1.25 to 1.25
- proj_bias: bfloat16 [384], P('dp'), may hold values from -3 to 3
- fc1_weight: bfloat16 [384, 1536], P('dp'), may hold values from -0.3125 to 0.3125
- fc1_bias: bfloat16 [1536], P('dp'), may hold values from -3 to 3
- fc2_weight: bfloat16 [1536, 384], P('dp'), may hold values from -0.15625 to 0.15625
- fc2_bias: bfloat16 [384], P('dp'), may hold values from -3 to 3
- cotangent: bfloat16 [768, 256, 384], P('dp'), may hold values from -6 to 6
Outputs:
- out_latents: bfloat16 [768, 256, 384], P('dp')
- grad_latents: float32 [768, 256, 384], P('dp')
- grad_conditioning: float32 [768, 384], P('dp')
- grad_ada_weight: float32 [384, 2304], P('dp')
- grad_ada_bias: float32 [2304], P('dp')
- grad_qkv_weight: float32 [384, 1152], P('dp')
- grad_qv_bias: float32 [2, 384], P(None, 'dp')
- grad_proj_weight: float32 [384, 384], P('dp')
- grad_proj_bias: float32 [384], P('dp')
- grad_fc1_weight: float32 [384, 1536], P('dp')
- grad_fc1_bias: float32 [1536], P('dp')
- grad_fc2_weight: float32 [1536, 384], P('dp')
- grad_fc2_bias: float32 [384], P('dp')
The draws below stay inside these ranges and needn't reach their ends.
Inputs may be any that keep to these rules, and one draw needn't show every extreme that they name: `latent_counts`: each device has 1 to 6 live latent slots, the first ones of its block; some device has exactly 6.
All inputs are finite; a program needn't handle non-finite values.
Results may differ from the reference program's by a relative error of at most 0.014.
The reference program's roundings to bfloat16 on the way count: a program that leaves them out, or rounds other values in their place, can miss the bound.
Values may be sent and summed in bfloat16 or wider, within the bound.
No kernel may reach another device: no remote copies, remote signals or barrier semaphores. Data moves between devices by JAX's collectives and lax.ppermute only.
A program may use at most 128 MiB of HBM per device.

```python
import jax
import jax.numpy as jnp
from jax import lax

D = 384
HEAD_DIM = 64
FF = 1536
S = 256
CAP = 6
LATENTS = 768
N_DP = 128


def draw_latent_counts(key, part):
    first_key, second_key = jax.random.split(jax.random.fold_in(key, 11))
    values = jax.random.randint(first_key, (N_DP,), 1, CAP + 1)
    chosen = jax.random.randint(second_key, (), 0, N_DP)
    return jnp.where(jnp.arange(N_DP) == chosen, CAP, values).astype(jnp.int32)


def block_scale(rng, shape, pieces, smallest, top_value):
    factor_of, own = 1.0, jax.random.fold_in(rng, 6)
    for axis_at, shards_of in pieces:
        heights = jnp.exp(jax.random.uniform(jax.random.fold_in(own, axis_at), (shards_of,), jnp.float32, smallest / len(pieces), top_value / len(pieces)))
        factor_of = factor_of * jnp.repeat(heights, shape[axis_at] // shards_of).reshape([-1 if axis == axis_at else 1 for axis in range(len(shape))])
    return factor_of


def gaussian(own_key, extent, deviation, reach, cuts=(), held_as=jnp.bfloat16):
    values = deviation * jax.random.normal(own_key, extent, jnp.float32)
    if cuts:
        values = values * block_scale(own_key, extent, cuts, -0.22, 0.18)
    return jnp.clip(values, -reach, reach).astype(held_as)


def setup_inputs(seed: int = 0) -> dict:
    key_of = jax.random.split(jax.random.key(seed), 15)
    return {
        "latents": gaussian(key_of[0], (LATENTS, S, D), 1.0, 6.0, ((0, 128),)),
        "conditioning": gaussian(key_of[1], (LATENTS, D), 1.0, 5.0, ((0, 128),)),
        "latent_counts": draw_latent_counts(jax.random.fold_in(key_of[14], 71), 0),
        "ada_weight": gaussian(key_of[3], (D, 6 * D), D ** -0.5, 0.3125, ((0, 128),)),
        "ada_bias": gaussian(key_of[4], (6 * D,), 0.5, 3.0, ((0, 128),)),
        "qkv_weight": gaussian(key_of[5], (D, 3 * D), D ** -0.5, 0.3125, ((0, 128),)),
        "qv_bias": gaussian(key_of[6], (2, D), 0.5, 3.0, ((1, 128),)),
        "proj_weight": gaussian(key_of[7], (D, D), (D // 16) ** -0.5, 1.25, ((0, 128),)),
        "proj_bias": gaussian(key_of[8], (D,), 0.5, 3.0, ((0, 128),)),
        "fc1_weight": gaussian(key_of[9], (D, FF), D ** -0.5, 0.3125, ((0, 128),)),
        "fc1_bias": gaussian(key_of[10], (FF,), 0.5, 3.0, ((0, 128),)),
        "fc2_weight": gaussian(key_of[11], (FF, D), FF ** -0.5, 0.15625, ((0, 128),)),
        "fc2_bias": gaussian(key_of[12], (D,), 0.5, 3.0, ((0, 128),)),
        "cotangent": gaussian(key_of[13], (LATENTS, S, D), 1.0, 6.0, ((0, 128),)),
    }


EPS = 1e-06

def layer_norm(values):
    centred = values - lax.optimization_barrier(jnp.mean(values, axis=-1, keepdims=True))
    inverse = lax.rsqrt(lax.optimization_barrier(jnp.mean(centred * centred, axis=-1, keepdims=True)) + EPS)
    return (centred * inverse, inverse)

def norm_back(upstream, normed, inverse):
    mean_up = lax.optimization_barrier(jnp.mean(upstream, axis=-1, keepdims=True))
    mean_prod = lax.optimization_barrier(jnp.mean(upstream * normed, axis=-1, keepdims=True))
    return (upstream - mean_up - normed * mean_prod) * inverse

def split_heads(matrix, heads):
    return jnp.transpose(matrix.reshape(matrix.shape[0], heads, -1), (1, 0, 2))

def join_heads(tensor):
    return jnp.transpose(tensor, (1, 0, 2)).reshape(tensor.shape[1], -1)

def contract(form, left, right):
    return jnp.einsum(form, left.astype(jnp.float32), right.astype(jnp.float32), precision=lax.Precision.HIGHEST)

def forward_latent(latent, cond_row, params):
    ada_w, ada_b, qkv_w, qv_b, proj_w, proj_b, first_w, first_b, second_w, second_b = params
    width = latent.shape[-1]
    heads = width // HEAD_DIM
    activated = jax.nn.silu(cond_row.astype(jnp.float32)).astype(jnp.bfloat16)
    modulation = jnp.dot(activated[None, :], ada_w, preferred_element_type=jnp.float32)[0] + ada_b.astype(jnp.float32)
    inputs = latent.astype(jnp.float32)
    normed_one, inverse_one = layer_norm(inputs)
    scale_one = modulation[width:2 * width]
    hidden_one = (normed_one * (1.0 + scale_one) + modulation[:width]).astype(jnp.bfloat16)
    bias_all = jnp.concatenate([qv_b[0], jnp.zeros_like(qv_b[0]), qv_b[1]]).astype(jnp.float32)
    projected = (jnp.dot(hidden_one, qkv_w, preferred_element_type=jnp.float32) + bias_all).astype(jnp.bfloat16)
    queries = split_heads(projected[:, :width], heads)
    keys_all = split_heads(projected[:, width:2 * width], heads)
    values_all = split_heads(projected[:, 2 * width:], heads)
    scores = contract('hqd,hkd->hqk', queries, keys_all) * HEAD_DIM ** (-0.5)
    row_max = lax.optimization_barrier(jnp.max(scores, axis=-1, keepdims=True))
    exponent = jnp.exp(scores - row_max)
    row_total = lax.optimization_barrier(jnp.sum(exponent, axis=-1, keepdims=True))
    log_sum = row_max + jnp.log(row_total)
    soft_weights = (exponent / row_total).astype(jnp.bfloat16)
    attended = join_heads(contract('hqk,hkd->hqd', soft_weights, values_all)).astype(jnp.bfloat16)
    branch_one = jnp.dot(attended, proj_w, preferred_element_type=jnp.float32) + proj_b.astype(jnp.float32)
    middle = inputs + modulation[2 * width:3 * width] * branch_one
    normed_two, inverse_two = layer_norm(middle)
    hidden_two = (normed_two * (1.0 + modulation[4 * width:5 * width]) + modulation[3 * width:4 * width]).astype(jnp.bfloat16)
    pre_act = jnp.dot(hidden_two, first_w, preferred_element_type=jnp.float32) + first_b.astype(jnp.float32)
    activ_two = jax.nn.gelu(pre_act, approximate=True).astype(jnp.bfloat16)
    branch_two = jnp.dot(activ_two, second_w, preferred_element_type=jnp.float32) + second_b.astype(jnp.float32)
    result = middle + modulation[5 * width:] * branch_two
    kept_values = (activated, modulation, normed_one, inverse_one, hidden_one, queries, keys_all, values_all, log_sum, attended, branch_one, normed_two, inverse_two, hidden_two, pre_act, activ_two, branch_two)
    return (result, kept_values)

def backward_latent(cond_row, params, kept_values, cotan_row):
    ada_w, ada_b, qkv_w, qv_b, proj_w, proj_b, first_w, first_b, second_w, second_b = params
    activated, modulation, normed_one, inverse_one, hidden_one, queries, keys_all, values_all, log_sum, attended, branch_one, normed_two, inverse_two, hidden_two, pre_act, activ_two, branch_two = kept_values
    width = modulation.shape[0] // 6
    heads = width // HEAD_DIM
    scale_one = modulation[width:2 * width]
    gate_one = modulation[2 * width:3 * width]
    scale_two = modulation[4 * width:5 * width]
    gate_two = modulation[5 * width:]
    grad_out = cotan_row.astype(jnp.float32)
    d_gate_two = lax.optimization_barrier(jnp.sum(grad_out * branch_two, axis=0))
    d_branch_two = grad_out * gate_two
    d_branch_two_b = d_branch_two.astype(jnp.bfloat16)
    grad_second = jnp.dot(activ_two.T, d_branch_two_b, preferred_element_type=jnp.float32)
    grad_second_bias = lax.optimization_barrier(jnp.sum(d_branch_two, axis=0))
    d_activ = jnp.dot(d_branch_two_b, second_w.T, preferred_element_type=jnp.float32)
    unused_value, gelu_back = jax.vjp(lambda arg_value: jax.nn.gelu(arg_value, approximate=True), pre_act)
    d_pre = gelu_back(d_activ)[0]
    d_pre_b = d_pre.astype(jnp.bfloat16)
    grad_first = jnp.dot(hidden_two.T, d_pre_b, preferred_element_type=jnp.float32)
    grad_first_bias = lax.optimization_barrier(jnp.sum(d_pre, axis=0))
    d_hidden_two = jnp.dot(d_pre_b, first_w.T, preferred_element_type=jnp.float32)
    d_scale_two = lax.optimization_barrier(jnp.sum(d_hidden_two * normed_two, axis=0))
    d_shift_two = lax.optimization_barrier(jnp.sum(d_hidden_two, axis=0))
    d_middle = grad_out + norm_back(d_hidden_two * (1.0 + scale_two), normed_two, inverse_two)
    d_gate_one = lax.optimization_barrier(jnp.sum(d_middle * branch_one, axis=0))
    d_branch_one = d_middle * gate_one
    d_branch_one_b = d_branch_one.astype(jnp.bfloat16)
    grad_proj = jnp.dot(attended.T, d_branch_one_b, preferred_element_type=jnp.float32)
    grad_proj_bias = lax.optimization_barrier(jnp.sum(d_branch_one, axis=0))
    d_attended = jnp.dot(d_branch_one_b, proj_w.T, preferred_element_type=jnp.float32).astype(jnp.bfloat16)
    d_heads = split_heads(d_attended, heads)
    scores = contract('hqd,hkd->hqk', queries, keys_all) * HEAD_DIM ** (-0.5)
    soft_full = jnp.exp(scores - log_sum)
    soft_b = soft_full.astype(jnp.bfloat16)
    d_values = contract('hqk,hqd->hkd', soft_b, d_heads)
    d_soft = contract('hqd,hkd->hqk', d_heads, values_all)
    row_delta = lax.optimization_barrier(jnp.sum(soft_full * d_soft, axis=-1, keepdims=True))
    d_scores = (soft_full * (d_soft - row_delta) * HEAD_DIM ** (-0.5)).astype(jnp.bfloat16)
    d_queries = join_heads(contract('hqk,hkd->hqd', d_scores, keys_all))
    d_keys = join_heads(contract('hqk,hqd->hkd', d_scores, queries))
    d_values = join_heads(d_values)
    d_projected = jnp.concatenate([d_queries, d_keys, d_values], axis=1).astype(jnp.bfloat16)
    grad_qkv = jnp.dot(hidden_one.T, d_projected, preferred_element_type=jnp.float32)
    grad_qv = jnp.stack([lax.optimization_barrier(jnp.sum(d_queries, axis=0)), lax.optimization_barrier(jnp.sum(d_values, axis=0))])
    d_hidden_one = jnp.dot(d_projected, qkv_w.T, preferred_element_type=jnp.float32)
    d_scale_one = lax.optimization_barrier(jnp.sum(d_hidden_one * normed_one, axis=0))
    d_shift_one = lax.optimization_barrier(jnp.sum(d_hidden_one, axis=0))
    grad_inputs = d_middle + norm_back(d_hidden_one * (1.0 + scale_one), normed_one, inverse_one)
    d_modulation = jnp.concatenate([d_shift_one, d_scale_one, d_gate_one, d_shift_two, d_scale_two, d_gate_two])
    grad_ada = activated.astype(jnp.float32)[:, None] * d_modulation[None, :]
    d_activated = jnp.dot(ada_w.astype(jnp.float32), d_modulation, precision=lax.Precision.HIGHEST)
    cond_float = cond_row.astype(jnp.float32)
    sigmoid_c = jax.nn.sigmoid(cond_float)
    grad_cond = d_activated * sigmoid_c * (1.0 + cond_float * (1.0 - sigmoid_c))
    grads = (grad_ada, d_modulation, grad_qkv, grad_qv, grad_proj, grad_proj_bias, grad_first, grad_first_bias, grad_second, grad_second_bias)
    return (grad_inputs, grad_cond, grads)

def reference(latents, conditioning, latent_counts, ada_weight, ada_bias, qkv_weight, qv_bias, proj_weight, proj_bias, fc1_weight, fc1_bias, fc2_weight, fc2_bias, cotangent):
    params = (ada_weight, ada_bias, qkv_weight, qv_bias, proj_weight, proj_bias, fc1_weight, fc1_bias, fc2_weight, fc2_bias)
    positions = jnp.arange(latents.shape[0], dtype=jnp.int32)
    live_flags = positions % CAP < latent_counts[positions // CAP]
    zero_grads = tuple((jnp.zeros(item.shape, jnp.float32) for item in params))

    def live_branch(operands):
        latent, cond_row, cotan_row = operands
        result, kept_values = forward_latent(latent, cond_row, params)
        grad_inputs, grad_cond, grads = backward_latent(cond_row, params, kept_values, cotan_row)
        return (result.astype(jnp.bfloat16), grad_inputs, grad_cond, grads)

    def dead_branch(operands):
        latent, cond_row, cotan_row = operands
        return (jnp.zeros(latent.shape, jnp.bfloat16), jnp.zeros(latent.shape, jnp.float32), jnp.zeros(cond_row.shape, jnp.float32), zero_grads)

    def step_latent(totals, item):
        latent, cond_row, cotan_row, flag = item
        result, grad_inputs, grad_cond, grads = lax.cond(flag, live_branch, dead_branch, (latent, cond_row, cotan_row))
        totals = tuple((left + right for left, right in zip(totals, grads)))
        return (totals, (result, grad_inputs, grad_cond))
    totals, stacked = lax.scan(step_latent, zero_grads, (latents, conditioning, cotangent, live_flags))
    return (stacked[0], stacked[1], stacked[2], totals[0], totals[1], totals[2], totals[3], totals[4], totals[5], totals[6], totals[7], totals[8], totals[9])
```

```python
import functools

import jax
import jax.numpy as jnp
from jax import lax
from jax.experimental import pallas as pl
from jax.experimental.pallas import tpu as pltpu
from jax.sharding import Mesh
from jax.sharding import PartitionSpec as P

F32 = jnp.float32
BF = jnp.bfloat16
EPS = 1e-06
D = 384
FF = 1536
S = 256
CAP = 6
HEADS = 6
ROWS = 16
LANES = 1408
GROUPS = 8
CHIPS = 64
K0 = 0.7978845608028654
K1 = K0 * 0.044715

PIECES = {"qkv": 9, "proj": 3, "ada": 18, "fc1": 12}


def slot_table():
    table, at = {}, 0
    for name, count in PIECES.items():
        places = []
        for _ in range(count):
            places.append((at // 5, at % 5) if at < 40 else (8 + at - 40, 4))
            at += 1
        table[name] = places
    return table


SLOTS = slot_table()
BIAS = {
    "ada": (0, 18, 3641, 16),
    "q": (18, 3, 21846, 16),
    "v": (21, 3, 21846, 16),
    "proj": (24, 3, 21846, 16),
    "fc1": (27, 12, 5462, 16),
    "fc2": (39, 3, 21846, 16),
}


def nn(a, b):
    return lax.dot_general(a, b, (((1,), (0,)), ((), ())), preferred_element_type=F32)


def nt(a, b):
    return lax.dot_general(a, b, (((1,), (1,)), ((), ())), preferred_element_type=F32)


def tn(a, b):
    return lax.dot_general(a, b, (((0,), (0,)), ((), ())), preferred_element_type=F32)


def iota(shape, dim):
    return lax.broadcasted_iota(jnp.int32, shape, dim)


def target_row(q, core, twelve):
    local = 2 * jnp.bitwise_and(jnp.right_shift(q, 4), 7) + jnp.where(q < 128, core, 1 - core)
    s = jnp.bitwise_and(q, 15)
    m = jnp.right_shift(s * 11, 5)
    if twelve:
        low = jnp.where(s < 12, 12 * local + s, 192 + 3 * local + s - 12)
    else:
        low = m * 48 + 3 * local + s - 3 * m
    return jnp.where(s < 15, low, 240 + local)


def selector(core, twelve, packed_dim):
    q = iota((256, 256), packed_dim)
    r = iota((256, 256), 1 - packed_dim)
    return jnp.where(target_row(q, core, twelve) == r, 1.0, 0.0).astype(BF)


def owner_of(name, shape):
    first, values, mult, shift = BIAS[name]
    n = iota(shape, 1)
    owner = jnp.right_shift(n * mult, shift)
    return owner, first + n - owner * values


def bias_row(rows_t, name, width):
    owner, _ = owner_of(name, (128, width))
    onehot = jnp.where(owner == iota((128, width), 0), 1.0, 0.0).astype(BF)
    spread = nn(rows_t, onehot)
    _, place = owner_of(name, (128, width))
    return jnp.sum(jnp.where(place == iota((128, width), 0), spread, 0.0), axis=0, keepdims=True)


def bias_block(value, name, width):
    owner, place = owner_of(name, (128, width))
    at = iota((128, width), 0)
    onehot = jnp.where(owner == at, 1.0, 0.0).astype(BF)
    spread = jnp.where(place == at, value, 0.0).astype(BF)
    return nt(onehot, spread)


def layer_norm(v):
    centred = v - jnp.mean(v, axis=-1, keepdims=True)
    inverse = lax.rsqrt(jnp.mean(centred * centred, axis=-1, keepdims=True) + EPS)
    return centred * inverse, inverse


def norm_back(e, n, r):
    return (e - jnp.mean(e, axis=-1, keepdims=True) - n * jnp.mean(e * n, axis=-1, keepdims=True)) * r


def pack_kernel(ada_ref, qkv_ref, proj_ref, fc1_ref, fc2_ref, bias_ref, out_ref, scr):
    scr[...] = jnp.zeros_like(scr)
    for name, ref in (("qkv", qkv_ref), ("proj", proj_ref), ("ada", ada_ref), ("fc1", fc1_ref)):
        for c, (t, m) in enumerate(SLOTS[name]):
            scr[3 * m : 3 * m + 3, t * 128 : t * 128 + 128] = ref[:, c * 128 : c * 128 + 128].astype(F32)
    scr[0:12, 1024:1408] = fc2_ref[...].astype(F32)
    scr[15:16, 0:128] = bias_ref[...].astype(F32)
    out_ref[...] = scr[...].astype(BF)


def unpack_kernel(in_ref, ada_ref, qkv_ref, proj_ref, fc1_ref, fc2_ref, bias_ref, scr):
    def add(i, _):
        scr[...] += in_ref[pl.ds(i, 1)][0].astype(F32)
        return 0

    scr[...] = jnp.zeros_like(scr)
    lax.fori_loop(0, CHIPS, add, 0, unroll=4)
    for name, ref in (("qkv", qkv_ref), ("proj", proj_ref), ("ada", ada_ref), ("fc1", fc1_ref)):
        for c, (t, m) in enumerate(SLOTS[name]):
            ref[:, c * 128 : c * 128 + 128] = scr[3 * m : 3 * m + 3, t * 128 : t * 128 + 128]
    fc2_ref[...] = scr[0:12, 1024:1408]
    bias_ref[...] = scr[15:16, 0:128]


def block_kernel(
    meta,
    x_ref,
    g_ref,
    cond_ref,
    wk_ref,
    ws_ref,
    out_ref,
    gx_ref,
    dcond_ref,
    ok_ref,
    os_ref,
    w_ada,
    w_qkv,
    w_proj,
    w_fc1,
    w_fc2,
    b_dev,
    b_qkv,
    b_proj,
    b_fc1,
    b_fc2,
    act_s,
    mod_s,
    dmod_s,
    a_qkv,
    a_proj,
    a_fc1,
    a_fc2t,
    s_bq,
    s_bv,
    s_bproj,
    s_bfc1,
    s_bfc2,
    n1_s,
    x1_s,
    n2_s,
    br_s,
    h1t_s,
    qkv_s,
    kt_s,
    vt_s,
    attt_s,
    p_s,
    act2_s,
    du_s,
    dqt_s,
    dqkv_s,
    stage,
    g_ada,
    g_fc2,
):
    slot = pl.program_id(0)
    count = meta[0]
    core = meta[1]
    weights = {"qkv": w_qkv, "proj": w_proj, "ada": w_ada, "fc1": w_fc1}

    @pl.when(slot == 0)
    def _():
        sel_a = selector(core, False, 1)
        sel_b = selector(core, True, 1)

        def unpack(g, _):
            rows = pl.ds(pl.multiple_of(g * 128, 128), 128)
            block = jnp.concatenate([wk_ref[rows, :], ws_ref[rows, :]], axis=0)
            low = nn(sel_a, block[:, :1024]).astype(BF)
            high = nn(sel_b, block[:, 1024:]).astype(BF)
            to48 = pl.ds(pl.multiple_of(g * 48, 16), 48)
            for name, ref in weights.items():
                for c, (t, m) in enumerate(SLOTS[name]):
                    if t < 8:
                        piece = low[48 * m : 48 * m + 48, t * 128 : t * 128 + 128]
                    else:
                        piece = high[192:240, (t - 8) * 128 : (t - 7) * 128]
                    ref[to48, c * 128 : c * 128 + 128] = piece
            w_fc2[pl.ds(pl.multiple_of(g * 192, 16), 192), :] = high[0:192, :]
            b_dev[pl.ds(pl.multiple_of(g * 16, 16), 16), :] = low[240:256, 0:128]
            return 0

        lax.fori_loop(0, GROUPS, unpack, 0)
        rows_t = b_dev[...].astype(F32).T.astype(BF)
        b_qkv[...] = jnp.concatenate(
            [bias_row(rows_t, "q", D), jnp.zeros((1, D), F32), bias_row(rows_t, "v", D)], axis=1
        )
        b_proj[...] = bias_row(rows_t, "proj", D)
        b_fc1[...] = bias_row(rows_t, "fc1", FF)
        b_fc2[...] = bias_row(rows_t, "fc2", D)
        act_s[...] = jnp.zeros_like(act_s)
        c = cond_ref[...].astype(F32)
        act_s[0:CAP, :] = c * jax.nn.sigmoid(c)
        mod_s[...] = nn(act_s[...].astype(BF), w_ada[...]) + bias_row(rows_t, "ada", 6 * D)
        for ref in (dmod_s, a_qkv, a_proj, a_fc1, a_fc2t, s_bq, s_bv, s_bproj, s_bfc1, s_bfc2):
            ref[...] = jnp.zeros_like(ref)

    @pl.when(slot >= count)
    def _():
        out_ref[...] = jnp.zeros_like(out_ref)
        gx_ref[...] = jnp.zeros_like(gx_ref)

    @pl.when(slot < count)
    def _():
        def mod(k):
            return mod_s[pl.ds(slot, 1), k * D : (k + 1) * D]

        x = x_ref[0].astype(F32)
        n1, r1 = layer_norm(x)
        n1_s[...] = n1
        h1 = (n1 * (1.0 + mod(1)) + mod(0)).astype(BF)
        h1t_s[...] = h1.T
        qkv_s[...] = (nn(h1, w_qkv[...]) + b_qkv[...]).astype(BF)
        qt = (qkv_s[:, 0:D] * 0.125).astype(BF).T
        kt_s[...] = qkv_s[:, D : 2 * D].T
        vt_s[...] = qkv_s[:, 2 * D : 3 * D].T
        none = jnp.zeros((64, S), BF)
        for h in range(HEADS):
            pair = (h // 2) * 128
            own = qt[h * 64 : h * 64 + 64, :]
            wide = jnp.concatenate([own, none] if h % 2 == 0 else [none, own], axis=0)
            s = nn(qkv_s[:, D + pair : D + pair + 128], wide)
            e = jnp.exp(s - jnp.max(s, axis=0, keepdims=True))
            p = e * (1.0 / jnp.sum(e, axis=0, keepdims=True))
            p_s[h] = p
            attt_s[h * 64 : h * 64 + 64, :] = nn(vt_s[h * 64 : h * 64 + 64, :], p.astype(BF)).astype(BF)
        branch = nn(attt_s[...].T, w_proj[...]) + b_proj[...]
        br_s[...] = branch
        x1 = x_ref[0].astype(F32) + mod(2) * branch
        x1_s[...] = x1
        n2, r2 = layer_norm(x1)
        n2_s[...] = n2
        h2 = (n2 * (1.0 + mod(4)) + mod(3)).astype(BF)
        dm = g_ref[0].astype(F32) * mod(5)
        s_bfc2[...] += jnp.sum(dm, axis=0, keepdims=True)
        dmb = dm.astype(BF)
        for c in range(6):
            at = slice(c * 256, c * 256 + 256)
            u = nn(h2, w_fc1[:, at]) + b_fc1[:, at]
            uu = u * u
            t = jnp.tanh(u * (K0 + K1 * uu))
            half = 0.5 + 0.5 * t
            act2_s[:, at] = (u * half).astype(BF)
            slope = half + 0.5 * u * (1.0 - t * t) * (K0 + (3.0 * K1) * uu)
            du = nt(dmb, w_fc2[at, :]) * slope
            s_bfc1[:, at] += jnp.sum(du, axis=0, keepdims=True)
            du_s[:, at] = du.astype(BF)
        m = nn(act2_s[...], w_fc2[...]) + b_fc2[...]
        out_ref[0] = (x1_s[...] + mod(5) * m).astype(BF)
        row = pl.ds(slot, 1)
        g = g_ref[0].astype(F32)
        dmod_s[row, 5 * D : 6 * D] = jnp.sum(g * m, axis=0, keepdims=True)
        a_fc2t[...] += nn(dmb.T, act2_s[...])
        a_fc1[...] += nn(h2.T, du_s[...])
        dh2 = nt(du_s[...], w_fc1[...])
        n2 = n2_s[...]
        dmod_s[row, 4 * D : 5 * D] = jnp.sum(dh2 * n2, axis=0, keepdims=True)
        dmod_s[row, 3 * D : 4 * D] = jnp.sum(dh2, axis=0, keepdims=True)
        dx1 = g_ref[0].astype(F32) + norm_back(dh2 * (1.0 + mod(4)), n2, r2)
        x1_s[...] = dx1
        dmod_s[row, 2 * D : 3 * D] = jnp.sum(dx1 * br_s[...], axis=0, keepdims=True)
        da = dx1 * mod(2)
        s_bproj[...] += jnp.sum(da, axis=0, keepdims=True)
        dab = da.astype(BF)
        a_proj[...] += nn(attt_s[...], dab)
        dot_ = nt(w_proj[...], dab).astype(BF)
        do = nt(dab, w_proj[...]).astype(BF)
        low = iota((S, 128), 1) < 64
        zero = jnp.zeros((S, 128), BF)
        for pair in range(3):
            at = slice(pair * 128, pair * 128 + 128)
            v_pair = qkv_s[:, 2 * D + pair * 128 : 2 * D + pair * 128 + 128]
            q_pair = (qkv_s[:, at] * 0.125).astype(BF)
            do_pair = do[:, at]
            dk = dv = None
            for e in range(2):
                h = 2 * pair + e
                own = dot_[h * 64 : h * 64 + 64, :]
                wide = jnp.concatenate([own, none] if e == 0 else [none, own], axis=0)
                dp = nn(v_pair, wide)
                p = p_s[h]
                delta = jnp.sum(p * dp, axis=0, keepdims=True)
                ds = (p * (dp - delta)).astype(BF)
                mine = low if e == 0 else jnp.logical_not(low)
                dv_h = nn(p.astype(BF), jnp.where(mine, do_pair, zero))
                dk_h = nn(ds, jnp.where(mine, q_pair, zero))
                dv = dv_h if dv is None else dv + dv_h
                dk = dk_h if dk is None else dk + dk_h
                dqt_s[h * 64 : h * 64 + 64, :] = nn(kt_s[h * 64 : h * 64 + 64, :], ds) * 0.125
            s_bv[:, at] += jnp.sum(dv, axis=0, keepdims=True)
            dqkv_s[:, D + pair * 128 : D + pair * 128 + 128] = dk.astype(BF)
            dqkv_s[:, 2 * D + pair * 128 : 2 * D + pair * 128 + 128] = dv.astype(BF)
        dqt = dqt_s[...]
        s_bq[...] += dqt[:, 0:128] + dqt[:, 128:256]
        dqkv_s[:, 0:D] = dqt.astype(BF).T
        a_qkv[...] += nn(h1t_s[...], dqkv_s[...])
        dh1 = nt(dqkv_s[...], w_qkv[...])
        n1 = n1_s[...]
        dmod_s[row, D : 2 * D] = jnp.sum(dh1 * n1, axis=0, keepdims=True)
        dmod_s[row, 0:D] = jnp.sum(dh1, axis=0, keepdims=True)
        gx_ref[0] = x1_s[...] + norm_back(dh1 * (1.0 + mod(1)), n1, r1)

    @pl.when(slot == CAP - 1)
    def _():
        dmod = dmod_s[...]
        high = dmod.astype(BF)
        both = jnp.concatenate([high.astype(F32), dmod - high.astype(F32)], axis=0).astype(BF)
        act = act_s[...]
        twice = jnp.concatenate([act, act], axis=0).astype(BF)
        g_ada[...] = tn(twice, both).astype(BF)
        dact = nt(both, w_ada[...])
        dact = (dact[0:8, :] + dact[8:16, :])[0:CAP, :]
        c = cond_ref[...].astype(F32)
        sig = jax.nn.sigmoid(c)
        dcond_ref[...] = dact * sig * (1.0 + c * (1.0 - sig))
        g_fc2[...] = a_fc2t[...].T.astype(BF)
        s_q = jnp.sum(s_bq[...].T, axis=0, keepdims=True)
        biases = bias_block(jnp.sum(dmod, axis=0, keepdims=True), "ada", 6 * D)
        for value, name, width in (
            (s_q, "q", D),
            (s_bv[...], "v", D),
            (s_bproj[...], "proj", D),
            (s_bfc1[...], "fc1", FF),
            (s_bfc2[...], "fc2", D),
        ):
            biases += bias_block(value, name, width)
        b_dev[...] = biases.astype(BF)
        stage[...] = jnp.zeros_like(stage)
        sel_a = selector(core, False, 0)
        sel_b = selector(core, True, 0)
        grads = {"qkv": a_qkv, "proj": a_proj, "ada": g_ada, "fc1": a_fc1}

        def pack(g, _):
            at48 = pl.ds(pl.multiple_of(g * 48, 16), 48)
            for name, ref in grads.items():
                for c, (t, m) in enumerate(SLOTS[name]):
                    stage[48 * m : 48 * m + 48, t * 128 : t * 128 + 128] = ref[
                        at48, c * 128 : c * 128 + 128
                    ].astype(BF)
            stage[0:192, 1024:1408] = g_fc2[pl.ds(pl.multiple_of(g * 192, 16), 192), :]
            stage[240:256, 0:128] = b_dev[pl.ds(pl.multiple_of(g * 16, 16), 16), :]
            rows = pl.ds(pl.multiple_of(g * 128, 128), 128)
            low_part = nn(sel_a, stage[:, 0:1024]).astype(BF)
            high_part = nn(sel_b, stage[:, 1024:1408]).astype(BF)
            ok_ref[rows, 0:1024] = low_part[0:128, :]
            os_ref[rows, 0:1024] = low_part[128:256, :]
            ok_ref[rows, 1024:1408] = high_part[0:128, :]
            os_ref[rows, 1024:1408] = high_part[128:256, :]
            return 0

        lax.fori_loop(0, GROUPS, pack, 0)


def whole(shape):
    return pl.BlockSpec(shape, lambda *_: (0,) * len(shape), pipeline_mode=pl.Buffered(1))


def run_block(meta, latents, cotangent, conditioning, mine, other):
    per_slot = pl.BlockSpec((1, S, D), lambda i, _: (i, 0, 0))
    packed = (CHIPS * ROWS, LANES)
    vm = pltpu.VMEM
    return pl.pallas_call(
        block_kernel,
        grid_spec=pltpu.PrefetchScalarGridSpec(
            num_scalar_prefetch=1,
            grid=(CAP,),
            in_specs=[per_slot, per_slot, whole((CAP, D)), whole(packed), whole(packed)],
            out_specs=[per_slot, per_slot, whole((CAP, D)), whole(packed), whole(packed)],
            scratch_shapes=[
                vm((D, 6 * D), BF),
                vm((D, 3 * D), BF),
                vm((D, D), BF),
                vm((D, FF), BF),
                vm((FF, D), BF),
                vm((128, 128), BF),
                vm((1, 3 * D), F32),
                vm((1, D), F32),
                vm((1, FF), F32),
                vm((1, D), F32),
                vm((8, D), F32),
                vm((8, 6 * D), F32),
                vm((8, 6 * D), F32),
                vm((D, 3 * D), F32),
                vm((D, D), F32),
                vm((D, FF), F32),
                vm((D, FF), F32),
                vm((D, 128), F32),
                vm((1, D), F32),
                vm((1, D), F32),
                vm((1, FF), F32),
                vm((1, D), F32),
                vm((S, D), F32),
                vm((S, D), F32),
                vm((S, D), F32),
                vm((S, D), F32),
                vm((D, S), BF),
                vm((S, 3 * D), BF),
                vm((D, S), BF),
                vm((D, S), BF),
                vm((D, S), BF),
                vm((HEADS, S, S), F32),
                vm((S, FF), BF),
                vm((S, FF), BF),
                vm((D, S), F32),
                vm((S, 3 * D), BF),
                vm((256, LANES), BF),
                vm((D, 6 * D), BF),
                vm((FF, D), BF),
            ],
        ),
        out_shape=[
            jax.ShapeDtypeStruct((CAP, S, D), BF),
            jax.ShapeDtypeStruct((CAP, S, D), F32),
            jax.ShapeDtypeStruct((CAP, D), F32),
            jax.ShapeDtypeStruct(packed, BF),
            jax.ShapeDtypeStruct(packed, BF),
        ],
        compiler_params=pltpu.CompilerParams(vmem_limit_bytes=56 << 20),
        name="block",
    )(meta, latents, cotangent, conditioning, mine, other)


def run_pack(ada, qkv, proj, fc1, fc2, biases):
    return pl.pallas_call(
        pack_kernel,
        out_shape=jax.ShapeDtypeStruct((ROWS, LANES), BF),
        scratch_shapes=[pltpu.VMEM((ROWS, LANES), F32)],
        name="pack",
    )(ada, qkv, proj, fc1, fc2, biases)


def run_unpack(blocks):
    shapes = ((3, 6 * D), (3, 3 * D), (3, D), (3, FF), (12, D), (1, 128))
    return pl.pallas_call(
        unpack_kernel,
        out_shape=[jax.ShapeDtypeStruct(s, F32) for s in shapes],
        scratch_shapes=[pltpu.VMEM((ROWS, LANES), F32)],
        name="unpack",
    )(blocks)


def per_device(
    latents,
    conditioning,
    latent_counts,
    ada_weight,
    ada_bias,
    qkv_weight,
    qv_bias,
    proj_weight,
    proj_bias,
    fc1_weight,
    fc1_bias,
    fc2_weight,
    fc2_bias,
    cotangent,
):
    chips = ("x", "y", "z")
    swap = [(0, 1), (1, 0)]
    biases = jnp.concatenate([ada_bias, qv_bias.reshape(-1), proj_bias, fc1_bias, fc2_bias])
    biases = jnp.pad(biases, (0, 128 - biases.shape[0])).reshape(1, 128)
    own = run_pack(ada_weight, qkv_weight, proj_weight, fc1_weight, fc2_weight, biases)
    mine = lax.all_to_all(jnp.broadcast_to(own[None], (CHIPS, ROWS, LANES)), chips, 0, 0, tiled=True)
    other = lax.ppermute(mine, "c", swap)
    core = lax.axis_index("c").astype(jnp.int32)
    meta = jnp.stack([latent_counts[0], core])
    flat = (CHIPS * ROWS, LANES)
    out, grad_x, grad_cond, keep, send = run_block(
        meta, latents, cotangent, conditioning, mine.reshape(flat), other.reshape(flat)
    )
    got = lax.ppermute(send, "c", swap)
    pair = (keep.astype(F32) + got.astype(F32)).astype(BF).reshape(CHIPS, ROWS, LANES)
    blocks = lax.all_to_all(pair, chips, 0, 0, tiled=True)
    ada, qkv, proj, fc1, fc2, small = run_unpack(blocks)
    small = small[0]
    return (
        out,
        grad_x,
        grad_cond,
        ada,
        small[0:18],
        qkv,
        small[18:24].reshape(2, 3),
        proj,
        small[24:27],
        fc1,
        small[27:39],
        fc2,
        small[39:42],
    )


def solution(mesh):
    cube = Mesh(mesh.devices.reshape(4, 4, 4, 2), ("x", "y", "z", "c"))
    dp = ("x", "y", "z", "c")
    weight = P(dp, None)
    tokens = P(dp, None, None)
    vector = P(dp)
    split = P(None, dp)
    return jax.shard_map(
        per_device,
        mesh=cube,
        in_specs=(
            tokens, weight, vector, weight, vector, weight, split,
            weight, vector, weight, vector, weight, vector, tokens,
        ),
        out_specs=(
            tokens, tokens, weight, weight, vector, weight, split,
            weight, vector, weight, vector, weight, vector,
        ),
        check_vma=False,
    )
```

```python
import functools

import jax
import jax.numpy as jnp
from jax import lax
from jax.experimental import pallas as pl
from jax.experimental.pallas import tpu as pltpu
from jax.sharding import Mesh
from jax.sharding import PartitionSpec as P

F32 = jnp.float32
BF = jnp.bfloat16
EPS = 1e-06
D = 384
FF = 1536
S = 256
CAP = 6
HEADS = 6
ROWS = 16
LANES = 1408
GROUPS = 8
CHIPS = 64
K0 = 0.7978845608028654
K1 = K0 * 0.044715

PIECES = {"qkv": 9, "proj": 3, "ada": 18, "fc1": 12}


def slot_table():
    table, at = {}, 0
    for name, count in PIECES.items():
        places = []
        for _ in range(count):
            places.append((at // 5, at % 5) if at < 40 else (8 + at - 40, 4))
            at += 1
        table[name] = places
    return table


SLOTS = slot_table()
BIAS = {
    "ada": (0, 18, 3641, 16),
    "q": (18, 3, 21846, 16),
    "v": (21, 3, 21846, 16),
    "proj": (24, 3, 21846, 16),
    "fc1": (27, 12, 5462, 16),
    "fc2": (39, 3, 21846, 16),
}


def nn(a, b):
    return lax.dot_general(a, b, (((1,), (0,)), ((), ())), preferred_element_type=F32)


def nt(a, b):
    return lax.dot_general(a, b, (((1,), (1,)), ((), ())), preferred_element_type=F32)


def tn(a, b):
    return lax.dot_general(a, b, (((0,), (0,)), ((), ())), preferred_element_type=F32)


def iota(shape, dim):
    return lax.broadcasted_iota(jnp.int32, shape, dim)


def target_row(q, core, twelve):
    local = 2 * jnp.bitwise_and(jnp.right_shift(q, 4), 7) + jnp.where(q < 128, core, 1 - core)
    s = jnp.bitwise_and(q, 15)
    m = jnp.right_shift(s * 11, 5)
    if twelve:
        low = jnp.where(s < 12, 12 * local + s, 192 + 3 * local + s - 12)
    else:
        low = m * 48 + 3 * local + s - 3 * m
    return jnp.where(s < 15, low, 240 + local)


def selector(core, twelve, packed_dim):
    q = iota((256, 256), packed_dim)
    r = iota((256, 256), 1 - packed_dim)
    return jnp.where(target_row(q, core, twelve) == r, 1.0, 0.0).astype(BF)


def owner_of(name, shape):
    first, values, mult, shift = BIAS[name]
    n = iota(shape, 1)
    owner = jnp.right_shift(n * mult, shift)
    return owner, first + n - owner * values


def bias_row(rows_t, name, width):
    owner, _ = owner_of(name, (128, width))
    onehot = jnp.where(owner == iota((128, width), 0), 1.0, 0.0).astype(BF)
    spread = nn(rows_t, onehot)
    _, place = owner_of(name, (128, width))
    return jnp.sum(jnp.where(place == iota((128, width), 0), spread, 0.0), axis=0, keepdims=True)


def bias_block(value, name, width):
    owner, place = owner_of(name, (128, width))
    at = iota((128, width), 0)
    onehot = jnp.where(owner == at, 1.0, 0.0).astype(BF)
    spread = jnp.where(place == at, value, 0.0).astype(BF)
    return nt(onehot, spread)


def layer_norm(v):
    centred = v - jnp.mean(v, axis=-1, keepdims=True)
    inverse = lax.rsqrt(jnp.mean(centred * centred, axis=-1, keepdims=True) + EPS)
    return centred * inverse, inverse


def norm_back(e, n, r):
    return (e - jnp.mean(e, axis=-1, keepdims=True) - n * jnp.mean(e * n, axis=-1, keepdims=True)) * r


def pack_kernel(ada_ref, qkv_ref, proj_ref, fc1_ref, fc2_ref, *rest):
    bada_ref, bqv_ref, bproj_ref, bfc1_ref, bfc2_ref, out_ref, scr = rest
    scr[...] = jnp.zeros_like(scr)
    for name, ref in (("qkv", qkv_ref), ("proj", proj_ref), ("ada", ada_ref), ("fc1", fc1_ref)):
        for c, (t, m) in enumerate(SLOTS[name]):
            scr[3 * m : 3 * m + 3, t * 128 : t * 128 + 128] = ref[:, c * 128 : c * 128 + 128].astype(F32)
    scr[0:12, 1024:1408] = fc2_ref[...].astype(F32)
    for ref, at in ((bada_ref, 0), (bproj_ref, 24), (bfc1_ref, 27), (bfc2_ref, 39)):
        n = ref.shape[0]
        scr[15:16, at : at + n] = ref[...].astype(F32).reshape(1, n)
    scr[15:16, 18:21] = bqv_ref[0:1, :].astype(F32)
    scr[15:16, 21:24] = bqv_ref[1:2, :].astype(F32)
    out_ref[...] = scr[...].astype(BF)


def unpack_kernel(in_ref, ada_ref, qkv_ref, proj_ref, fc1_ref, fc2_ref, *rest):
    bada_ref, bqv_ref, bproj_ref, bfc1_ref, bfc2_ref, scr = rest
    def add(i, _):
        scr[...] += in_ref[pl.ds(i, 1)][0].astype(F32)
        return 0

    scr[...] = jnp.zeros_like(scr)
    lax.fori_loop(0, CHIPS, add, 0, unroll=4)
    for name, ref in (("qkv", qkv_ref), ("proj", proj_ref), ("ada", ada_ref), ("fc1", fc1_ref)):
        for c, (t, m) in enumerate(SLOTS[name]):
            ref[:, c * 128 : c * 128 + 128] = scr[3 * m : 3 * m + 3, t * 128 : t * 128 + 128]
    fc2_ref[...] = scr[0:12, 1024:1408]
    for ref, at in ((bada_ref, 0), (bproj_ref, 24), (bfc1_ref, 27), (bfc2_ref, 39)):
        n = ref.shape[0]
        ref[...] = scr[15:16, at : at + n].reshape(n)
    bqv_ref[0:1, :] = scr[15:16, 18:21]
    bqv_ref[1:2, :] = scr[15:16, 21:24]


def block_kernel(
    meta,
    x_ref,
    g_ref,
    cond_ref,
    wk_ref,
    ws_ref,
    out_ref,
    gx_ref,
    dcond_ref,
    ok_ref,
    os_ref,
    w_ada,
    w_qkv,
    w_proj,
    w_fc1,
    w_fc2,
    b_dev,
    b_qkv,
    b_proj,
    b_fc1,
    b_fc2,
    act_s,
    mod_s,
    dmod_s,
    a_qkv,
    a_proj,
    a_fc1,
    a_fc2t,
    s_bq,
    s_bv,
    s_bproj,
    s_bfc1,
    s_bfc2,
    n1_s,
    x1_s,
    n2_s,
    br_s,
    h1t_s,
    qkv_s,
    kt_s,
    vt_s,
    attt_s,
    p_s,
    da2_s,
    dmt_s,
    h2t_s,
    act2_s,
    du_s,
    dqt_s,
    dqkv_s,
    stage,
    g_ada,
    g_fc2,
):
    slot = pl.program_id(0)
    count = meta[0]
    core = meta[1]
    weights = {"qkv": w_qkv, "proj": w_proj, "ada": w_ada, "fc1": w_fc1}

    @pl.when(slot == 0)
    def _():
        sel_a = selector(core, False, 1)
        sel_b = selector(core, True, 1)

        def unpack(g, _):
            rows = pl.ds(pl.multiple_of(g * 128, 128), 128)
            block = jnp.concatenate([wk_ref[rows, :], ws_ref[rows, :]], axis=0)
            low = nn(sel_a, block[:, :1024]).astype(BF)
            high = nn(sel_b, block[:, 1024:]).astype(BF)
            to48 = pl.ds(pl.multiple_of(g * 48, 16), 48)
            for name, ref in weights.items():
                for c, (t, m) in enumerate(SLOTS[name]):
                    if t < 8:
                        piece = low[48 * m : 48 * m + 48, t * 128 : t * 128 + 128]
                    else:
                        piece = high[192:240, (t - 8) * 128 : (t - 7) * 128]
                    ref[to48, c * 128 : c * 128 + 128] = piece
            w_fc2[pl.ds(pl.multiple_of(g * 192, 16), 192), :] = high[0:192, :]
            b_dev[pl.ds(pl.multiple_of(g * 16, 16), 16), :] = low[240:256, 0:128]
            return 0

        lax.fori_loop(0, GROUPS, unpack, 0)
        rows_t = b_dev[...].astype(F32).T.astype(BF)
        b_qkv[...] = jnp.concatenate(
            [bias_row(rows_t, "q", D), jnp.zeros((1, D), F32), bias_row(rows_t, "v", D)], axis=1
        )
        b_proj[...] = bias_row(rows_t, "proj", D)
        b_fc1[...] = bias_row(rows_t, "fc1", FF)
        b_fc2[...] = bias_row(rows_t, "fc2", D)
        act_s[...] = jnp.zeros_like(act_s)
        c = cond_ref[...].astype(F32)
        act_s[0:CAP, :] = c * jax.nn.sigmoid(c)
        mod_s[...] = nn(act_s[...].astype(BF), w_ada[...]) + bias_row(rows_t, "ada", 6 * D)
        for ref in (dmod_s, a_qkv, a_proj, a_fc1, a_fc2t, s_bq, s_bv, s_bproj, s_bfc1, s_bfc2):
            ref[...] = jnp.zeros_like(ref)

    @pl.when(slot >= count)
    def _():
        out_ref[...] = jnp.zeros_like(out_ref)
        gx_ref[...] = jnp.zeros_like(gx_ref)

    @pl.when(slot < count)
    def _():
        def mod(k):
            return mod_s[pl.ds(slot, 1), k * D : (k + 1) * D]

        x = x_ref[0].astype(F32)
        n1, r1 = layer_norm(x)
        n1_s[...] = n1
        h1 = (n1 * (1.0 + mod(1)) + mod(0)).astype(BF)
        h1t_s[...] = h1.T
        qkv_s[...] = (nn(h1, w_qkv[...]) + b_qkv[...]).astype(BF)
        qt = (qkv_s[:, 0:D] * 0.125).astype(BF).T
        kt_s[...] = qkv_s[:, D : 2 * D].T
        vt_s[...] = qkv_s[:, 2 * D : 3 * D].T
        none = jnp.zeros((64, S), BF)
        dm = g_ref[0].astype(F32) * mod(5)
        s_bfc2[...] += jnp.sum(dm, axis=0, keepdims=True)
        dmb = dm.astype(BF)

        def scores(pair):
            at = pair * 128
            q0, q1 = qt[at : at + 64, :], qt[at + 64 : at + 128, :]
            wide = jnp.concatenate(
                [jnp.concatenate([q0, none], axis=0), jnp.concatenate([none, q1], axis=0)], axis=1
            )
            return nn(qkv_s[:, D + at : D + at + 128], wide)

        def attend(pair, p):
            at = pair * 128
            both = nn(vt_s[at : at + 128, :], p).astype(BF)
            attt_s[at : at + 64, :] = both[0:64, 0:S]
            attt_s[at + 64 : at + 128, :] = both[64:128, S : 2 * S]

        ahead, last = scores(0), None
        for pair in range(3):
            s = ahead
            if pair < 2:
                ahead = scores(pair + 1)
            if last is not None:
                attend(pair - 1, last)
            for c in (2 * pair, 2 * pair + 1):
                da2_s[:, c * 256 : c * 256 + 256] = nt(dmb, w_fc2[c * 256 : c * 256 + 256, :])
            e = jnp.exp(s - jnp.max(s, axis=0, keepdims=True))
            p = e * (1.0 / jnp.sum(e, axis=0, keepdims=True))
            p_s[pair] = p
            last = p.astype(BF)
        attend(2, last)
        branch = nn(attt_s[...].T, w_proj[...]) + b_proj[...]
        br_s[...] = branch
        x1 = x_ref[0].astype(F32) + mod(2) * branch
        x1_s[...] = x1
        n2, r2 = layer_norm(x1)
        n2_s[...] = n2
        h2 = (n2 * (1.0 + mod(4)) + mod(3)).astype(BF)
        for c in range(6):
            at = slice(c * 256, c * 256 + 256)
            u = nn(h2, w_fc1[:, at]) + b_fc1[:, at]
            uu = u * u
            t = jnp.tanh(u * (K0 + K1 * uu))
            half = 0.5 + 0.5 * t
            act2_s[:, at] = (u * half).astype(BF)
            slope = half + 0.5 * u * (1.0 - t * t) * (K0 + (3.0 * K1) * uu)
            du = da2_s[:, at] * slope
            s_bfc1[:, at] += jnp.sum(du, axis=0, keepdims=True)
            du_s[:, at] = du.astype(BF)
        m = nn(act2_s[...], w_fc2[...]) + b_fc2[...]
        out_ref[0] = (x1_s[...] + mod(5) * m).astype(BF)
        row = pl.ds(slot, 1)
        g = g_ref[0].astype(F32)
        dmod_s[row, 5 * D : 6 * D] = jnp.sum(g * m, axis=0, keepdims=True)
        dmt_s[...] = dmb.T
        h2t_s[...] = h2.T
        dh2 = nt(du_s[...], w_fc1[...])
        n2 = n2_s[...]
        dmod_s[row, 4 * D : 5 * D] = jnp.sum(dh2 * n2, axis=0, keepdims=True)
        dmod_s[row, 3 * D : 4 * D] = jnp.sum(dh2, axis=0, keepdims=True)
        dx1 = g_ref[0].astype(F32) + norm_back(dh2 * (1.0 + mod(4)), n2, r2)
        x1_s[...] = dx1
        dmod_s[row, 2 * D : 3 * D] = jnp.sum(dx1 * br_s[...], axis=0, keepdims=True)
        da = dx1 * mod(2)
        s_bproj[...] += jnp.sum(da, axis=0, keepdims=True)
        dab = da.astype(BF)
        a_proj[...] += nn(attt_s[...], dab)
        dot_ = nt(w_proj[...], dab).astype(BF)
        do = nt(dab, w_proj[...]).astype(BF)
        low = iota((S, 128), 1) < 64
        zero = jnp.zeros((S, 128), BF)
        def back_scores(pair):
            at = pair * 128
            d0, d1 = dot_[at : at + 64, :], dot_[at + 64 : at + 128, :]
            wide = jnp.concatenate(
                [jnp.concatenate([d0, none], axis=0), jnp.concatenate([none, d1], axis=0)], axis=1
            )
            return nn(qkv_s[:, 2 * D + at : 2 * D + at + 128], wide)

        def back_attend(pair, p, ds):
            at = slice(pair * 128, pair * 128 + 128)
            q_pair = (qkv_s[:, at] * 0.125).astype(BF)
            do_pair = do[:, at]
            do_two = jnp.concatenate([jnp.where(low, do_pair, zero), jnp.where(low, zero, do_pair)], axis=0)
            q_two = jnp.concatenate([jnp.where(low, q_pair, zero), jnp.where(low, zero, q_pair)], axis=0)
            dv = nn(p, do_two)
            dk = nn(ds, q_two)
            both = nn(kt_s[at, :], ds) * 0.125
            dqt_s[pair * 128 : pair * 128 + 64, :] = both[0:64, 0:S]
            dqt_s[pair * 128 + 64 : pair * 128 + 128, :] = both[64:128, S : 2 * S]
            s_bv[:, at] += jnp.sum(dv, axis=0, keepdims=True)
            dqkv_s[:, D + pair * 128 : D + pair * 128 + 128] = dk.astype(BF)
            dqkv_s[:, 2 * D + pair * 128 : 2 * D + pair * 128 + 128] = dv.astype(BF)

        ahead, last = back_scores(0), None
        for pair in range(3):
            dp = ahead
            if pair < 2:
                ahead = back_scores(pair + 1)
            if last is not None:
                back_attend(pair - 1, *last)
            third = slice(pair * 512, pair * 512 + 512)
            a_fc2t[:, third] += nn(dmt_s[...], act2_s[:, third])
            a_fc1[:, third] += nn(h2t_s[...], du_s[:, third])
            p = p_s[pair]
            delta = jnp.sum(p * dp, axis=0, keepdims=True)
            last = (p.astype(BF), (p * (dp - delta)).astype(BF))
        back_attend(2, *last)
        dqt = dqt_s[...]
        s_bq[...] += dqt[:, 0:128] + dqt[:, 128:256]
        dqkv_s[:, 0:D] = dqt.astype(BF).T
        a_qkv[...] += nn(h1t_s[...], dqkv_s[...])
        dh1 = nt(dqkv_s[...], w_qkv[...])
        n1 = n1_s[...]
        dmod_s[row, D : 2 * D] = jnp.sum(dh1 * n1, axis=0, keepdims=True)
        dmod_s[row, 0:D] = jnp.sum(dh1, axis=0, keepdims=True)
        gx_ref[0] = x1_s[...] + norm_back(dh1 * (1.0 + mod(1)), n1, r1)

    @pl.when(slot == CAP - 1)
    def _():
        dmod = dmod_s[...]
        high = dmod.astype(BF)
        both = jnp.concatenate([high.astype(F32), dmod - high.astype(F32)], axis=0).astype(BF)
        act = act_s[...]
        twice = jnp.concatenate([act, act], axis=0).astype(BF)
        g_ada[...] = tn(twice, both).astype(BF)
        dact = nt(both, w_ada[...])
        dact = (dact[0:8, :] + dact[8:16, :])[0:CAP, :]
        c = cond_ref[...].astype(F32)
        sig = jax.nn.sigmoid(c)
        dcond_ref[...] = dact * sig * (1.0 + c * (1.0 - sig))
        g_fc2[...] = a_fc2t[...].T.astype(BF)
        s_q = jnp.sum(s_bq[...].T, axis=0, keepdims=True)
        biases = bias_block(jnp.sum(dmod, axis=0, keepdims=True), "ada", 6 * D)
        for value, name, width in (
            (s_q, "q", D),
            (s_bv[...], "v", D),
            (s_bproj[...], "proj", D),
            (s_bfc1[...], "fc1", FF),
            (s_bfc2[...], "fc2", D),
        ):
            biases += bias_block(value, name, width)
        b_dev[...] = biases.astype(BF)
        stage[...] = jnp.zeros_like(stage)
        sel_a = selector(core, False, 0)
        sel_b = selector(core, True, 0)
        grads = {"qkv": a_qkv, "proj": a_proj, "ada": g_ada, "fc1": a_fc1}

        def pack(g, _):
            at48 = pl.ds(pl.multiple_of(g * 48, 16), 48)
            for name, ref in grads.items():
                for c, (t, m) in enumerate(SLOTS[name]):
                    stage[48 * m : 48 * m + 48, t * 128 : t * 128 + 128] = ref[
                        at48, c * 128 : c * 128 + 128
                    ].astype(BF)
            stage[0:192, 1024:1408] = g_fc2[pl.ds(pl.multiple_of(g * 192, 16), 192), :]
            stage[240:256, 0:128] = b_dev[pl.ds(pl.multiple_of(g * 16, 16), 16), :]
            rows = pl.ds(pl.multiple_of(g * 128, 128), 128)
            low_part = nn(sel_a, stage[:, 0:1024]).astype(BF)
            high_part = nn(sel_b, stage[:, 1024:1408]).astype(BF)
            ok_ref[rows, 0:1024] = low_part[0:128, :]
            os_ref[rows, 0:1024] = low_part[128:256, :]
            ok_ref[rows, 1024:1408] = high_part[0:128, :]
            os_ref[rows, 1024:1408] = high_part[128:256, :]
            return 0

        lax.fori_loop(0, GROUPS, pack, 0)


def whole(shape):
    return pl.BlockSpec(shape, lambda *_: (0,) * len(shape), pipeline_mode=pl.Buffered(1))


def resident():
    return pl.BlockSpec(memory_space=pltpu.VMEM)


def run_block(meta, latents, cotangent, conditioning, mine, other):
    per_slot = pl.BlockSpec((1, S, D), lambda i, _: (i, 0, 0))
    packed = (CHIPS * ROWS, LANES)
    vm = pltpu.VMEM
    return pl.pallas_call(
        block_kernel,
        grid_spec=pltpu.PrefetchScalarGridSpec(
            num_scalar_prefetch=1,
            grid=(CAP,),
            in_specs=[per_slot, per_slot, whole((CAP, D)), resident(), resident()],
            out_specs=[per_slot, per_slot, whole((CAP, D)), resident(), resident()],
            scratch_shapes=[
                vm((D, 6 * D), BF),
                vm((D, 3 * D), BF),
                vm((D, D), BF),
                vm((D, FF), BF),
                vm((FF, D), BF),
                vm((128, 128), BF),
                vm((1, 3 * D), F32),
                vm((1, D), F32),
                vm((1, FF), F32),
                vm((1, D), F32),
                vm((8, D), F32),
                vm((8, 6 * D), F32),
                vm((8, 6 * D), F32),
                vm((D, 3 * D), F32),
                vm((D, D), F32),
                vm((D, FF), F32),
                vm((D, FF), F32),
                vm((D, 128), F32),
                vm((1, D), F32),
                vm((1, D), F32),
                vm((1, FF), F32),
                vm((1, D), F32),
                vm((S, D), F32),
                vm((S, D), F32),
                vm((S, D), F32),
                vm((S, D), F32),
                vm((D, S), BF),
                vm((S, 3 * D), BF),
                vm((D, S), BF),
                vm((D, S), BF),
                vm((D, S), BF),
                vm((3, S, 2 * S), F32),
                vm((S, FF), F32),
                vm((D, S), BF),
                vm((D, S), BF),
                vm((S, FF), BF),
                vm((S, FF), BF),
                vm((D, S), F32),
                vm((S, 3 * D), BF),
                vm((256, LANES), BF),
                vm((D, 6 * D), BF),
                vm((FF, D), BF),
            ],
        ),
        out_shape=[
            jax.ShapeDtypeStruct((CAP, S, D), BF),
            jax.ShapeDtypeStruct((CAP, S, D), F32),
            jax.ShapeDtypeStruct((CAP, D), F32),
            jax.ShapeDtypeStruct(packed, BF),
            jax.ShapeDtypeStruct(packed, BF),
        ],
        compiler_params=pltpu.CompilerParams(vmem_limit_bytes=40 << 20),
        name="block",
    )(meta, latents, cotangent, conditioning, mine, other)


def run_pack(*shards):
    return pl.pallas_call(
        pack_kernel,
        out_shape=jax.ShapeDtypeStruct((ROWS, LANES), BF),
        scratch_shapes=[pltpu.VMEM((ROWS, LANES), F32)],
        name="pack",
    )(*shards)


def run_unpack(blocks):
    shapes = ((3, 6 * D), (3, 3 * D), (3, D), (3, FF), (12, D), (18,), (2, 3), (3,), (12,), (3,))
    return pl.pallas_call(
        unpack_kernel,
        out_shape=[jax.ShapeDtypeStruct(s, F32) for s in shapes],
        scratch_shapes=[pltpu.VMEM((ROWS, LANES), F32)],
        name="unpack",
    )(blocks)


def per_device(
    latents,
    conditioning,
    latent_counts,
    ada_weight,
    ada_bias,
    qkv_weight,
    qv_bias,
    proj_weight,
    proj_bias,
    fc1_weight,
    fc1_bias,
    fc2_weight,
    fc2_bias,
    cotangent,
):
    chips = ("x", "y", "z")
    swap = [(0, 1), (1, 0)]
    own = run_pack(
        ada_weight, qkv_weight, proj_weight, fc1_weight, fc2_weight,
        ada_bias, qv_bias, proj_bias, fc1_bias, fc2_bias,
    )
    mine = lax.all_to_all(jnp.broadcast_to(own[None], (CHIPS, ROWS, LANES)), chips, 0, 0, tiled=True)
    other = lax.ppermute(mine, "c", swap)
    core = lax.axis_index("c").astype(jnp.int32)
    meta = jnp.stack([latent_counts[0], core])
    flat = (CHIPS * ROWS, LANES)
    out, grad_x, grad_cond, keep, send = run_block(
        meta, latents, cotangent, conditioning, mine.reshape(flat), other.reshape(flat)
    )
    got = lax.ppermute(send, "c", swap)
    pair = (keep.astype(F32) + got.astype(F32)).astype(BF).reshape(CHIPS, ROWS, LANES)
    blocks = lax.all_to_all(pair, chips, 0, 0, tiled=True)
    ada, qkv, proj, fc1, fc2, bada, bqv, bproj, bfc1, bfc2 = run_unpack(blocks)
    return out, grad_x, grad_cond, ada, bada, qkv, bqv, proj, bproj, fc1, bfc1, fc2, bfc2


def solution(mesh):
    cube = Mesh(mesh.devices.reshape(4, 4, 4, 2), ("x", "y", "z", "c"))
    dp = ("x", "y", "z", "c")
    weight = P(dp, None)
    tokens = P(dp, None, None)
    vector = P(dp)
    split = P(None, dp)
    return jax.shard_map(
        per_device,
        mesh=cube,
        in_specs=(
            tokens, weight, vector, weight, vector, weight, split,
            weight, vector, weight, vector, weight, vector, tokens,
        ),
        out_specs=(
            tokens, tokens, weight, weight, vector, weight, split,
            weight, vector, weight, vector, weight, vector,
        ),
        check_vma=False,
    )
```
